512 devices in a mesh: rows: 64 (over x, y, z_lo), cols: 8 (over z_hi, core).
Axes of the slice: x: 4, y: 8, z: 8 (z_hi: 4, z_lo: 2; z = z_hi * 2 + z_lo), core: 2. Of those that a mesh axis runs over, the one named last changes fastest.
Arguments:
- design: float32 [65536, 4096], P('rows', 'cols')
- signs: int32 [65536], P('rows'), may hold values from -1 to 1, as said below
- response: float32 [65536], P('rows'), may hold values from -6 to 6
- picks: int32 [8192], replicated, may hold values from 0 to 65535, as said below
Outputs:
- gram_blocks: float32 [512, 8, 512], P('rows', 'cols')
- rhs: float32 [4096], P('cols')
The draws below stay inside these ranges and needn't reach their ends.
Inputs may be any that keep to these rules, and one draw needn't show every extreme that they name: `signs`: every entry is +1 or -1. `picks`: strictly increasing, all distinct; the first and the last row are always sampled.
All inputs are finite; a program needn't handle non-finite values.
Results may differ from the reference program's by a relative error of at most 0.0003.
Values sent between devices are 32-bit elements; how exact they have to be, the bound alone decides.
A program may use at most 64 MiB of HBM per device.

```python
import jax
import jax.numpy as jnp
from jax import lax

D = 4096
BW = 512
NROWS = 65536
SAMPLES = 8192


def row_signs(key):
    return (2 * jax.random.randint(jax.random.fold_in(key, 11), (NROWS,), 0, 2) - 1).astype(jnp.int32)


def draw_design(key, part):
    flips = row_signs(key).astype(jnp.float32)
    noise = jax.random.normal(key, (NROWS, D + 1), jnp.float32)
    ramp = 10.0 ** (jnp.arange(D, dtype=jnp.float32) / D)
    column_scale = ramp * jax.random.uniform(jax.random.fold_in(key, 1), (D,), jnp.float32, 0.7, 1.4)
    row_scale = jnp.exp(jax.random.uniform(jax.random.fold_in(key, 2), (NROWS,), jnp.float32, 0.0, 2.302585))
    values = noise[:, :D] + 0.5 * noise[:, 1:] + 0.1 * flips[:, None]
    return (values * column_scale[None, :] * row_scale[:, None]).astype(jnp.float32)


def draw_signs(key, part):
    return row_signs(key)


def draw_picks(key, part):
    inner = 1 + jax.random.permutation(key, NROWS - 2)[:SAMPLES - 2]
    ends = jnp.array([0, NROWS - 1], dtype=jnp.int32)
    return jnp.sort(jnp.concatenate([ends, inner.astype(jnp.int32)])).astype(jnp.int32)


def level_of(stream_key, dims, cuts, low, high):
    loudness = 1.0
    for axis_at, shards_of in cuts:
        heights = jax.random.uniform(jax.random.fold_in(jax.random.fold_in(stream_key, 6), axis_at), (shards_of,), jnp.float32, low / len(cuts), high / len(cuts))
        loudness = loudness * jnp.repeat(jnp.exp(heights), dims[axis_at] // shards_of).reshape((-1,) + (1,) * (len(dims) - 1 - axis_at))
    return loudness


def gaussian(rng, extent, scale, reach, shards=(), kind=jnp.bfloat16):
    values = jax.random.normal(rng, extent, jnp.float32) * scale
    if len(shards) > 0:
        values = level_of(rng, extent, shards, -0.22, 0.18) * values
    return jnp.clip(values, min=-reach, max=reach).astype(kind)


def setup_inputs(seed: int = 0) -> dict:
    streams_of = jax.random.split(jax.random.key(seed), 5)
    design = draw_design(jax.random.fold_in(streams_of[4], 71), 0)
    signs = draw_signs(jax.random.fold_in(streams_of[4], 71), 0)
    response = gaussian(streams_of[2], (NROWS,), 1.0, 6.0, ((0, 64),), jnp.float32)
    picks = draw_picks(jax.random.fold_in(streams_of[4], 71), 0)
    return {"design": design, "signs": signs, "response": response, "picks": picks}


epsilon = 1e-06

def hadamard_rows(values):
    total = values.shape[0]
    stride = 1
    while stride < total:
        folded = values.reshape((total // (2 * stride), 2, stride) + values.shape[1:])
        values = jnp.stack([folded[:, 0] + folded[:, 1], folded[:, 0] - folded[:, 1]], axis=1).reshape(values.shape)
        stride = stride * 2
    return values

def reference(design, signs, response, picks):
    flips = signs.astype(jnp.float32)
    mixed = hadamard_rows(design * flips[:, None])
    mixed_response = hadamard_rows(response * flips)
    chosen = mixed[picks]
    chosen_response = mixed_response[picks]
    mean_diag = jnp.sum(chosen * chosen) / D + epsilon
    power = jnp.sum(chosen_response * chosen_response)
    blocks = chosen.reshape(SAMPLES, D // BW, BW)
    gram = jnp.einsum('sbi,sbj->ibj', blocks, blocks, precision=lax.Precision.HIGHEST)
    rhs_sum = jnp.dot(chosen_response, chosen, precision=lax.Precision.HIGHEST)
    gram_blocks = gram / mean_diag
    rhs = rhs_sum * jnp.sqrt(jnp.float32(SAMPLES)) / jnp.sqrt(mean_diag * power)
    return (gram_blocks, rhs)
```

```python
import jax
import jax.numpy as jnp
from jax import lax
from jax.sharding import PartitionSpec as P

D = 4096
BW = 512

epsilon = 1e-06


def sylvester(order, dtype):
    row_ids = lax.broadcasted_iota(jnp.int32, (order, order), 0)
    col_ids = lax.broadcasted_iota(jnp.int32, (order, order), 1)
    common = jnp.bitwise_and(row_ids, col_ids)
    return (1 - 2 * jnp.bitwise_and(lax.population_count(common), 1)).astype(dtype)


def halves(values):
    top = lax.reduce_precision(values, 8, 7)
    rest = values - top
    return top.astype(jnp.bfloat16), rest.astype(jnp.bfloat16)


def thirds(values):
    top = lax.reduce_precision(values, 8, 7)
    rest = values - top
    mid = lax.reduce_precision(rest, 8, 7)
    low = rest - mid
    return tuple(part.astype(jnp.bfloat16) for part in (top, mid, low))


def dot(left, right):
    return jnp.dot(left, right, preferred_element_type=jnp.float32)


def mix(order, values):
    matrix = sylvester(order, jnp.bfloat16)
    return sum(dot(matrix, part) for part in halves(values))


def local(design, signs, response, picks):
    height, width = design.shape
    groups = lax.axis_size("rows")
    position = lax.axis_index("rows")
    share = height // groups
    flips = signs.astype(jnp.float32)

    whole = lax.all_gather(response * flips, "rows", axis=0, tiled=True)
    side = 256
    square = whole.reshape(side, side)
    h_side = sylvester(side, jnp.bfloat16)
    square = sum(dot(h_side, part) for part in thirds(square))
    square = sum(dot(part, h_side) for part in thirds(square))
    answer = square.reshape(groups, groups, share)
    answer = lax.dynamic_slice_in_dim(answer, position, 1, axis=1)[:, 0, :]

    mixed = mix(height, design * flips[:, None])
    mixed = lax.all_to_all(
        mixed.reshape(groups, share, width), "rows", split_axis=0, concat_axis=0, tiled=True
    )
    mixed = mix(groups, mixed.reshape(groups, share * width)).reshape(height, width)

    group_of = picks // height
    inside = picks % height - position * share
    of_group = (lax.iota(jnp.int32, groups)[:, None] == group_of[None, :]).astype(jnp.bfloat16)
    of_local = (inside[:, None] == lax.iota(jnp.int32, share)[None, :]).astype(jnp.bfloat16)
    picked = dot(of_group, of_local)

    picked_answer = picked * answer
    chosen = mixed * picked.reshape(height)[:, None]
    top, rest = halves(chosen)

    def outer(left, right):
        return lax.dot_general(left, right, (((0,), (0,)), ((), ())), preferred_element_type=jnp.float32)

    cross = outer(top, rest)
    gram = outer(top, top) + cross + cross.T
    rhs_part = jnp.sum(chosen * picked_answer.reshape(height)[:, None], axis=0)
    power_part = jnp.sum(picked_answer * picked_answer)
    trace_part = jnp.sum(chosen * chosen)
    trace_sum = lax.psum(trace_part, ("rows", "cols"))

    blocks = gram.reshape(groups, BW // groups, width)
    extra = jnp.stack([rhs_part, jnp.full((width,), power_part)])
    extra = jnp.broadcast_to(extra[None], (groups, 2, width))
    parts = jnp.concatenate([blocks, extra], axis=1)
    parts = lax.all_to_all(parts, "rows", split_axis=0, concat_axis=0, tiled=True)
    sums = jnp.sum(parts, axis=0)

    mean_diag = trace_sum / D + epsilon
    gram_blocks = sums[: BW // groups, None, :] / mean_diag
    samples = picks.shape[0]
    rhs = sums[BW // groups] * jnp.sqrt(jnp.float32(samples)) / jnp.sqrt(mean_diag * sums[BW // groups + 1])
    return (gram_blocks, rhs)


def solution(mesh):
    in_specs = (P("rows", "cols"), P("rows"), P("rows"), P())
    out_specs = (P("rows", "cols", None), P("cols"))
    return jax.shard_map(local, mesh=mesh, in_specs=in_specs, out_specs=out_specs, check_vma=False)
```

```python
import functools

import jax
import jax.numpy as jnp
from jax import lax
from jax.experimental import pallas as pl
from jax.experimental.pallas import tpu as pltpu
from jax.sharding import PartitionSpec as P

D = 4096
BW = 512

epsilon = 1e-06


def sylvester(order, dtype):
    row_ids = lax.broadcasted_iota(jnp.int32, (order, order), 0)
    col_ids = lax.broadcasted_iota(jnp.int32, (order, order), 1)
    common = jnp.bitwise_and(row_ids, col_ids)
    return (1 - 2 * jnp.bitwise_and(lax.population_count(common), 1)).astype(dtype)


def halves(values):
    top = lax.reduce_precision(values, 8, 7)
    rest = values - top
    return top.astype(jnp.bfloat16), rest.astype(jnp.bfloat16)


def dot(left, right):
    return jnp.dot(left, right, preferred_element_type=jnp.float32)


def mix(order, values):
    matrix = sylvester(order, jnp.bfloat16)
    return sum(dot(matrix, part) for part in halves(values))


MESH = pl.DeviceIdType.MESH
VMEM = pltpu.VMEM
LANES = 128


def peer(groups, k):
    me = lax.axis_index("rows")
    x = lax.rem(me // 16 + k // 16, groups // 16)
    y = lax.rem(lax.rem(me // 2, 8) + lax.rem(k, 8), 8)
    z = lax.rem(lax.rem(me, 2) + lax.rem(k // 8, 2), 2)
    return x * 16 + y * 2 + z


def each_peer(groups, action):
    def step(k, carry):
        action(peer(groups, k))
        return carry

    lax.fori_loop(1, groups, step, 0)


def to_row(source, landing, sends, receives, slot, there):
    return pltpu.make_async_remote_copy(
        src_ref=source,
        dst_ref=landing.at[slot],
        send_sem=sends.at[there],
        recv_sem=receives.at[slot],
        device_id={"rows": there},
        device_id_type=MESH,
    )


def greet_rows(groups):
    barrier = pltpu.get_barrier_semaphore()
    each_peer(
        groups,
        lambda there: pl.semaphore_signal(barrier, inc=1, device_id={"rows": there}, device_id_type=MESH),
    )
    return barrier


def trade_kernel(groups, mixed, answer, mixed_out, answer_out, sends, receives, answer_sends, answer_receives, own):
    me = lax.axis_index("rows")
    pl.semaphore_wait(greet_rows(groups), groups - 1)

    def start(there):
        to_row(mixed.at[there], mixed_out, sends, receives, me, there).start()
        to_row(answer.at[there], answer_out, answer_sends, answer_receives, me, there).start()

    def finish(there):
        to_row(mixed.at[there], mixed_out, sends, receives, there, there).wait()
        to_row(answer.at[there], answer_out, answer_sends, answer_receives, there, there).wait()

    each_peer(groups, start)
    keep = pltpu.make_async_copy(mixed.at[me], mixed_out.at[me], own.at[0])
    keep_answer = pltpu.make_async_copy(answer.at[me], answer_out.at[me], own.at[1])
    keep.start()
    keep_answer.start()
    keep.wait()
    keep_answer.wait()
    each_peer(groups, finish)


def trade(mixed, answer):
    groups = mixed.shape[0]
    return pl.pallas_call(
        functools.partial(trade_kernel, groups),
        out_shape=[
            jax.ShapeDtypeStruct(mixed.shape, jnp.float32),
            jax.ShapeDtypeStruct(answer.shape, jnp.float32),
        ],
        in_specs=[pl.BlockSpec(memory_space=VMEM)] * 2,
        out_specs=[pl.BlockSpec(memory_space=VMEM)] * 2,
        scratch_shapes=[pltpu.SemaphoreType.DMA((groups,))] * 4 + [pltpu.SemaphoreType.DMA((2,))],
        compiler_params=pltpu.CompilerParams(collective_id=0, has_side_effects=True),
    )(mixed, answer)


def finish_kernel(
    groups, columns, samples, gram, small, gram_out, rhs_out,
    land, land_small, land_total, total,
    sends, receives, small_sends, small_receives, total_sends, total_receives, own,
):
    me = lax.axis_index("rows")
    column = lax.axis_index("cols")
    barrier = greet_rows(groups)
    for k in range(1, columns):
        there = lax.rem(column + k, columns)
        pl.semaphore_signal(barrier, inc=1, device_id={"cols": there}, device_id_type=MESH)
    pl.semaphore_wait(barrier, groups + columns - 2)

    each_peer(groups, lambda there: to_row(small, land_small, small_sends, small_receives, me, there).start())
    each_peer(groups, lambda there: to_row(gram.at[there], land, sends, receives, me, there).start())
    keep = pltpu.make_async_copy(gram.at[me], land.at[me], own.at[0])
    keep_small = pltpu.make_async_copy(small, land_small.at[me], own.at[1])
    keep.start()
    keep_small.start()
    keep.wait()
    keep_small.wait()
    each_peer(groups, lambda there: to_row(small, land_small, small_sends, small_receives, there, there).wait())
    total[...] = jnp.sum(land_small[...], axis=0)

    def to_column(slot, there):
        return pltpu.make_async_remote_copy(
            src_ref=total,
            dst_ref=land_total.at[slot],
            send_sem=total_sends.at[there],
            recv_sem=total_receives.at[slot],
            device_id={"cols": there},
            device_id_type=MESH,
        )

    for k in range(1, columns):
        to_column(column, lax.rem(column + k, columns)).start()
    each_peer(groups, lambda there: to_row(gram.at[there], land, sends, receives, there, there).wait())
    sums = jnp.sum(land[...], axis=0)
    mine = total[...]
    trace = mine[4:5, :]
    for k in range(1, columns):
        there = lax.rem(column + k, columns)
        to_column(there, there).wait()
        trace = trace + land_total[there][4:5, :]
    mean_diag = trace / D + epsilon
    for j in range(BW // LANES):
        gram_out[:, j * LANES:(j + 1) * LANES] = sums[:, j * LANES:(j + 1) * LANES] / mean_diag
    rhs_out[...] = mine * jnp.sqrt(jnp.float32(samples)) / jnp.sqrt(mean_diag * mine[5:6, :])


def finish(gram, small, columns, samples):
    groups, height, width = gram.shape
    return pl.pallas_call(
        functools.partial(finish_kernel, groups, columns, samples),
        out_shape=[
            jax.ShapeDtypeStruct((height, width), jnp.float32),
            jax.ShapeDtypeStruct(small.shape, jnp.float32),
        ],
        in_specs=[pl.BlockSpec(memory_space=VMEM)] * 2,
        out_specs=[pl.BlockSpec(memory_space=VMEM)] * 2,
        scratch_shapes=[
            VMEM(gram.shape, jnp.float32),
            VMEM((groups,) + small.shape, jnp.float32),
            VMEM((columns,) + small.shape, jnp.float32),
            VMEM(small.shape, jnp.float32),
        ]
        + [pltpu.SemaphoreType.DMA((groups,))] * 4
        + [pltpu.SemaphoreType.DMA((columns,))] * 2
        + [pltpu.SemaphoreType.DMA((2,))],
        compiler_params=pltpu.CompilerParams(collective_id=1, has_side_effects=True),
    )(gram, small)


def local(design, signs, response, picks):
    height, width = design.shape
    groups = lax.axis_size("rows")
    position = lax.axis_index("rows")
    share = height // groups
    flips = signs.astype(jnp.float32)

    exact = lax.Precision.HIGHEST
    h_32 = sylvester(32, jnp.float32)
    answer = jnp.dot(h_32, (response * flips).reshape(32, 32), precision=exact)
    answer = jnp.dot(answer, h_32, precision=exact).reshape(groups, 1, share)
    answer = jnp.pad(answer, ((0, 0), (0, 0), (0, LANES - share)))

    mixed = mix(height, design * flips[:, None])
    mixed, answer = trade(mixed.reshape(groups, share, width), answer)
    mixed = mix(groups, mixed.reshape(groups, share * width)).reshape(height, width)
    answer = jnp.dot(sylvester(groups, jnp.float32), answer[:, 0, :share], precision=exact)

    group_of = picks // height
    inside = picks % height - position * share
    of_group = (lax.iota(jnp.int32, groups)[:, None] == group_of[None, :]).astype(jnp.bfloat16)
    of_local = (inside[:, None] == lax.iota(jnp.int32, share)[None, :]).astype(jnp.bfloat16)
    picked = dot(of_group, of_local)

    picked_answer = picked * answer
    chosen = mixed * picked.reshape(height)[:, None]
    top, rest = halves(chosen)

    def outer(left, right):
        return lax.dot_general(left, right, (((0,), (0,)), ((), ())), preferred_element_type=jnp.float32)

    cross = outer(top, rest)
    gram = outer(top, top) + cross + cross.T
    rhs_part = jnp.sum(chosen * picked_answer.reshape(height)[:, None], axis=0)
    power_part = jnp.sum(picked_answer * picked_answer)
    trace_part = jnp.sum(chosen * chosen)
    small = jnp.concatenate([
        rhs_part.reshape(BW // LANES, LANES),
        jnp.full((1, LANES), trace_part),
        jnp.full((1, LANES), power_part),
        jnp.zeros((2, LANES), jnp.float32),
    ])
    gram_rows, small = finish(
        gram.reshape(groups, BW // groups, width), small, lax.axis_size("cols"), picks.shape[0]
    )
    return (gram_rows[:, None, :], small[: BW // LANES].reshape(BW))


def solution(mesh):
    in_specs = (P("rows", "cols"), P("rows"), P("rows"), P())
    out_specs = (P("rows", "cols", None), P("cols"))
    return jax.shard_map(local, mesh=mesh, in_specs=in_specs, out_specs=out_specs, check_vma=False)
```

```python
import functools

import jax
import jax.numpy as jnp
from jax import lax
from jax.experimental import pallas as pl
from jax.experimental.pallas import tpu as pltpu
from jax.sharding import PartitionSpec as P

D = 4096
BW = 512

epsilon = 1e-06


def sylvester(order, dtype):
    row_ids = lax.broadcasted_iota(jnp.int32, (order, order), 0)
    col_ids = lax.broadcasted_iota(jnp.int32, (order, order), 1)
    common = jnp.bitwise_and(row_ids, col_ids)
    return (1 - 2 * jnp.bitwise_and(lax.population_count(common), 1)).astype(dtype)


def halves(values):
    top = values.astype(jnp.bfloat16)
    return top, (values - top.astype(jnp.float32)).astype(jnp.bfloat16)


def dot(left, right):
    return jnp.dot(left, right, preferred_element_type=jnp.float32)


def butterfly(values):
    apart = 1
    while apart < len(values):
        values = [
            values[i ^ apart] - values[i] if i & apart else values[i] + values[i ^ apart]
            for i in range(len(values))
        ]
        apart *= 2
    return values


MESH = pl.DeviceIdType.MESH
VMEM = pltpu.VMEM
LANES = 128


def peer(groups, k):
    me = lax.axis_index("rows")
    x = lax.rem(me // 16 + k // 16, groups // 16)
    y = lax.rem(lax.rem(me // 2, 8) + lax.rem(k, 8), 8)
    z = lax.rem(lax.rem(me, 2) + lax.rem(k // 8, 2), 2)
    return x * 16 + y * 2 + z


def each_peer(groups, action):
    def step(k, carry):
        action(peer(groups, k))
        return carry

    lax.fori_loop(1, groups, step, 0)


def to_row(source, landing, sends, receives, slot, there):
    return pltpu.make_async_remote_copy(
        src_ref=source,
        dst_ref=landing.at[slot],
        send_sem=sends.at[there],
        recv_sem=receives.at[slot],
        device_id={"rows": there},
        device_id_type=MESH,
    )


def greet_rows(groups):
    barrier = pltpu.get_barrier_semaphore()
    each_peer(
        groups,
        lambda there: pl.semaphore_signal(barrier, inc=1, device_id={"rows": there}, device_id_type=MESH),
    )
    return barrier


def trade_kernel(groups, mixed, answer, mixed_out, answer_out, sends, receives, answer_sends, answer_receives, own):
    me = lax.axis_index("rows")
    pl.semaphore_wait(greet_rows(groups), groups - 1)

    def start(there):
        to_row(mixed.at[there], mixed_out, sends, receives, me, there).start()
        to_row(answer.at[there // 8], answer_out, answer_sends, answer_receives, me, there).start()

    def finish(there):
        to_row(mixed.at[there], mixed_out, sends, receives, there, there).wait()
        to_row(answer.at[there // 8], answer_out, answer_sends, answer_receives, there, there).wait()

    each_peer(groups, start)
    keep = pltpu.make_async_copy(mixed.at[me], mixed_out.at[me], own.at[0])
    keep_answer = pltpu.make_async_copy(answer.at[me // 8], answer_out.at[me], own.at[1])
    keep.start()
    keep_answer.start()
    keep.wait()
    keep_answer.wait()
    each_peer(groups, finish)


def trade(mixed, answer):
    groups = mixed.shape[0]
    return pl.pallas_call(
        functools.partial(trade_kernel, groups),
        out_shape=[
            jax.ShapeDtypeStruct(mixed.shape, jnp.float32),
            jax.ShapeDtypeStruct((groups, 1, LANES), jnp.float32),
        ],
        in_specs=[pl.BlockSpec(memory_space=VMEM)] * 2,
        out_specs=[pl.BlockSpec(memory_space=VMEM)] * 2,
        scratch_shapes=[pltpu.SemaphoreType.DMA((groups,))] * 4 + [pltpu.SemaphoreType.DMA((2,))],
        compiler_params=pltpu.CompilerParams(collective_id=0, has_side_effects=True),
    )(mixed, answer)


def mix_kernel(design, signs, response, mixed, answer):
    height, width = design.shape
    blocks = height // LANES
    h_lanes = sylvester(LANES, jnp.float32)
    flips = signs[...].astype(jnp.float32)
    for b in range(blocks):
        top, rest = halves(design[b * LANES:(b + 1) * LANES, :])
        matrix = (h_lanes * flips[b:b + 1, :]).astype(jnp.bfloat16)
        part = dot(matrix, top) + dot(matrix, rest)
        mixed[b * 8:(b + 1) * 8] = part.reshape(8, LANES // 8, width)

    def level(i, carry):
        row = lax.rem(i, 2) * 8
        values = butterfly([mixed[b * 8 + i // 2, pl.ds(row, 8), :] for b in range(blocks)])
        for b in range(blocks):
            mixed[b * 8 + i // 2, pl.ds(row, 8), :] = values[b]
        return carry

    lax.fori_loop(0, LANES // 8, level, 0)
    folded = jnp.dot(response[...] * flips, h_lanes, precision=lax.Precision.HIGHEST, preferred_element_type=jnp.float32)
    rows = butterfly([folded[b:b + 1, :] for b in range(blocks)])
    for b in range(blocks):
        answer[b] = rows[b]


def local_mix(design, signs, response):
    height, width = design.shape
    blocks = height // LANES
    return pl.pallas_call(
        mix_kernel,
        out_shape=[
            jax.ShapeDtypeStruct((64, height // 64, width), jnp.float32),
            jax.ShapeDtypeStruct((blocks, 1, LANES), jnp.float32),
        ],
        in_specs=[pl.BlockSpec(memory_space=VMEM)] * 3,
        out_specs=[pl.BlockSpec(memory_space=VMEM)] * 2,
    )(design, signs.reshape(blocks, LANES), response.reshape(blocks, LANES))


def gram_kernel(mixed, answer, picks, gram, small, held):
    groups, share, width = mixed.shape
    height = groups * share
    position = lax.axis_index("rows")

    def first(i, carry):
        row = lax.rem(i, 2) * 8
        values = butterfly([mixed[i // 2 * 8 + b, pl.ds(row, 8), :] for b in range(8)])
        for b in range(8):
            held[i // 2 * 8 + b, pl.ds(row, 8), :] = values[b]
        return carry

    def second(i, carry):
        row = lax.rem(i, 2) * 8
        values = butterfly([held[b * 8 + i // 2, pl.ds(row, 8), :] for b in range(8)])
        for b in range(8):
            held[b * 8 + i // 2, pl.ds(row, 8), :] = values[b]
        return carry

    lax.fori_loop(0, 16, first, 0)
    lax.fori_loop(0, 16, second, 0)
    mixed_answer = jnp.dot(
        sylvester(groups, jnp.float32), answer[:, 0, :],
        precision=lax.Precision.HIGHEST, preferred_element_type=jnp.float32,
    )
    wanted = picks[...]
    group_of = jnp.right_shift(wanted, 10)
    inside = jnp.bitwise_and(wanted, height - 1) - position * share
    samples = wanted.shape[1]
    of_group = (lax.broadcasted_iota(jnp.int32, (groups, samples), 0) == group_of).astype(jnp.float32)
    of_local = (lax.broadcasted_iota(jnp.int32, (LANES, samples), 0) == inside).astype(jnp.float32)
    picked = lax.dot_general(
        of_group.astype(jnp.bfloat16), of_local[:share].astype(jnp.bfloat16), (((1,), (1,)), ((), ())),
        preferred_element_type=jnp.float32,
    )
    lane = lax.broadcasted_iota(jnp.int32, (groups, share, share), 2)
    local_row = lax.broadcasted_iota(jnp.int32, (groups, share, share), 1)
    picked_rows = jnp.sum(jnp.where(lane == local_row, picked[:, None, :], 0.0), axis=2, keepdims=True)
    lane = lax.broadcasted_iota(jnp.int32, (groups, share, LANES), 2)
    local_row = lax.broadcasted_iota(jnp.int32, (groups, share, LANES), 1) + lax.rem(position, 8) * share
    answer_rows = jnp.sum(jnp.where(lane == local_row, mixed_answer[:, None, :], 0.0), axis=2, keepdims=True)
    picked_rows = picked_rows.reshape(height, 1)
    answer_rows = answer_rows.reshape(height, 1) * picked_rows

    chosen = held[...].reshape(height, width) * picked_rows
    top, rest = halves(chosen)

    def outer(left, right):
        return lax.dot_general(left, right, (((0,), (0,)), ((), ())), preferred_element_type=jnp.float32)

    total = outer(top, top) + outer(top, rest) + outer(rest, top)
    half = width // 2
    for h in range(2):
        gram[h] = total[:, h * half:(h + 1) * half].reshape(gram.shape[1:])
    rhs = jnp.sum(chosen * answer_rows, axis=0, keepdims=True)
    trace = jnp.sum(jnp.sum(chosen * chosen, axis=0, keepdims=True), axis=1, keepdims=True)
    power = jnp.sum(answer_rows * answer_rows, axis=0, keepdims=True)
    for j in range(width // LANES):
        small[j:j + 1, :] = rhs[:, j * LANES:(j + 1) * LANES]
    small[4:5, :] = jnp.broadcast_to(trace, (1, LANES))
    small[5:6, :] = jnp.broadcast_to(power, (1, LANES))
    small[6:8, :] = jnp.zeros((2, LANES), jnp.float32)


def local_gram(mixed, answer, picks):
    groups, share, width = mixed.shape
    return pl.pallas_call(
        gram_kernel,
        out_shape=[
            jax.ShapeDtypeStruct((2, groups // 16, 8, 2, width // groups, width // 2), jnp.float32),
            jax.ShapeDtypeStruct((8, LANES), jnp.float32),
        ],
        in_specs=[pl.BlockSpec(memory_space=VMEM)] * 3,
        out_specs=[pl.BlockSpec(memory_space=VMEM)] * 2,
        scratch_shapes=[VMEM(mixed.shape, jnp.float32)],
        compiler_params=pltpu.CompilerParams(vmem_limit_bytes=60 * 2**20),
    )(mixed, answer, picks.reshape(1, -1))


def finish_kernel(
    columns, samples, gram, small, gram_out, rhs_out,
    a_first, a_first_sum, a_second, a_second_sum, a_third,
    b_first, b_first_sum, b_second, b_second_sum, b_third,
    s_first, s_first_sum, s_second, s_second_sum, s_third,
    sends, receives,
):
    me = lax.axis_index("rows")
    column = lax.axis_index("cols")
    along_x = gram.shape[1]
    x = me // 16
    y = lax.rem(me // 2, 8)
    z = lax.rem(me, 2)
    other_z = 1 - z

    def row_at(kx, ky, kz):
        return lax.rem(x + kx, along_x) * 16 + lax.rem(y + ky, 8) * 2 + lax.rem(z + kz, 2)

    plane = [(kx, kz) for kz in range(2) for kx in range(along_x) if kx or kz]
    plane_rows = [row_at(kx, 0, kz) for kx, kz in plane]
    y_rows = [row_at(0, ky, 0) for ky in range(1, 8)]
    others = [lax.rem(column + k, columns) for k in range(1, columns)]

    barrier = pltpu.get_barrier_semaphore()
    for there in plane_rows + y_rows:
        pl.semaphore_signal(barrier, inc=1, device_id={"rows": there}, device_id_type=MESH)
    for there in others:
        pl.semaphore_signal(barrier, inc=1, device_id={"cols": there}, device_id_type=MESH)
    pl.semaphore_wait(barrier, len(plane_rows) + len(y_rows) + len(others))

    used = []

    def send(source, landing, **there):
        index = len(used)
        used.append(index)
        copy = pltpu.make_async_remote_copy(
            src_ref=source,
            dst_ref=landing,
            send_sem=sends.at[index],
            recv_sem=receives.at[index],
            device_id=there,
            device_id_type=MESH,
        )
        copy.start()
        return copy

    def wait(copies):
        for copy in copies:
            copy.wait()

    s1 = [send(small, s_first.at[k], rows=there) for k, there in enumerate(plane_rows)]
    b1 = [send(gram.at[1, :, :, other_z], b_first, rows=row_at(0, 0, 1))]
    a1 = [
        send(gram.at[0, lax.rem(x + k, along_x)], a_first.at[k - 1], rows=row_at(k, 0, 0))
        for k in (2, 1, 3)
    ]
    wait(s1)
    s_first_sum[...] = small[...] + jnp.sum(s_first[...], axis=0)
    s2 = [send(s_first_sum, s_second.at[k], rows=there) for k, there in enumerate(y_rows)]
    wait(b1)
    b_first_sum[...] = gram[1, :, :, z] + b_first[...]
    b2 = [
        send(b_first_sum.at[lax.rem(x + k, along_x)], b_second.at[k - 1], rows=row_at(k, 0, 0))
        for k in (2, 1, 3)
    ]
    wait(a1)
    a_first_sum[...] = gram[0, x] + a_first[0] + a_first[1] + a_first[2]
    a2 = [send(a_first_sum.at[:, other_z], a_second, rows=row_at(0, 0, 1))]
    wait(s2)
    s_second_sum[...] = s_first_sum[...] + jnp.sum(s_second[...], axis=0)
    s3 = [send(s_second_sum, s_third.at[k], cols=there) for k, there in enumerate(others)]
    wait(a2)
    a_second_sum[...] = a_first_sum[:, z] + a_second[...]
    a3 = [
        send(a_second_sum.at[lax.rem(y + k, 8)], a_third.at[k - 1], rows=y_rows[k - 1])
        for k in (4, 3, 5, 2, 6, 1, 7)
    ]
    wait(b2)
    b_second_sum[...] = b_first_sum[x] + b_second[0] + b_second[1] + b_second[2]
    b3 = [
        send(b_second_sum.at[lax.rem(y + k, 8)], b_third.at[k - 1], rows=y_rows[k - 1])
        for k in (4, 3, 5, 2, 6, 1, 7)
    ]
    wait(s3)
    mine = s_second_sum[...]
    mean_diag = (mine + jnp.sum(s_third[...], axis=0))[4:5, :] / D + epsilon
    scaled = mine * jnp.sqrt(jnp.float32(samples)) / jnp.sqrt(mean_diag * mine[5:6, :])
    rhs_out[...] = scaled[: BW // LANES, :]
    wait(a3)
    left = a_second_sum[y] + jnp.sum(a_third[...], axis=0)
    wait(b3)
    right = b_second_sum[y] + jnp.sum(b_third[...], axis=0)
    for half, block in enumerate((left, right)):
        for j in range(BW // 2 // LANES):
            at = half * (BW // 2) + j * LANES
            gram_out[:, at:at + LANES] = block[:, j * LANES:(j + 1) * LANES] / mean_diag


def finish(gram, small, columns, samples):
    _, nx, ny, nz, height, half = gram.shape
    count = 2 * (nx - 1) + 2 + 2 * (ny - 1) + (nx * nz - 1) + (ny - 1) + (columns - 1)

    def space(*shape):
        return VMEM(shape, jnp.float32)

    tile = small.shape
    return pl.pallas_call(
        functools.partial(finish_kernel, columns, samples),
        out_shape=[
            jax.ShapeDtypeStruct((height, 2 * half), jnp.float32),
            jax.ShapeDtypeStruct((BW // LANES, LANES), jnp.float32),
        ],
        in_specs=[pl.BlockSpec(memory_space=VMEM)] * 2,
        out_specs=[pl.BlockSpec(memory_space=VMEM)] * 2,
        scratch_shapes=[
            space(nx - 1, ny, nz, height, half), space(ny, nz, height, half),
            space(ny, height, half), space(ny, height, half), space(ny - 1, height, half),
            space(nx, ny, height, half), space(nx, ny, height, half),
            space(nx - 1, ny, height, half), space(ny, height, half), space(ny - 1, height, half),
            space(nx * nz - 1, *tile), space(*tile), space(ny - 1, *tile), space(*tile), space(columns - 1, *tile),
            pltpu.SemaphoreType.DMA((count,)),
            pltpu.SemaphoreType.DMA((count,)),
        ],
        compiler_params=pltpu.CompilerParams(collective_id=1, has_side_effects=True),
    )(gram, small)


def local(design, signs, response, picks):
    mixed, answer = trade(*local_mix(design, signs, response))
    gram, small = local_gram(mixed, answer, picks)
    gram_rows, rhs = finish(gram, small, lax.axis_size("cols"), picks.shape[0])
    return (gram_rows[:, None, :], rhs.reshape(BW))


def solution(mesh):
    in_specs = (P("rows", "cols"), P("rows"), P("rows"), P())
    out_specs = (P("rows", "cols", None), P("cols"))
    return jax.shard_map(local, mesh=mesh, in_specs=in_specs, out_specs=out_specs, check_vma=False)
```

```python
import functools

import jax
import jax.numpy as jnp
from jax import lax
from jax.experimental import pallas as pl
from jax.experimental.pallas import tpu as pltpu
from jax.sharding import PartitionSpec as P

D = 4096
BW = 512

epsilon = 1e-06


def sylvester(order, dtype):
    row_ids = lax.broadcasted_iota(jnp.int32, (order, order), 0)
    col_ids = lax.broadcasted_iota(jnp.int32, (order, order), 1)
    common = jnp.bitwise_and(row_ids, col_ids)
    return (1 - 2 * jnp.bitwise_and(lax.population_count(common), 1)).astype(dtype)


def halves(values):
    top = values.astype(jnp.bfloat16)
    return top, (values - top.astype(jnp.float32)).astype(jnp.bfloat16)


def dot(left, right):
    return jnp.dot(left, right, preferred_element_type=jnp.float32)


def butterfly(values):
    apart = 1
    while apart < len(values):
        values = [
            values[i ^ apart] - values[i] if i & apart else values[i] + values[i ^ apart]
            for i in range(len(values))
        ]
        apart *= 2
    return values


MESH = pl.DeviceIdType.MESH
VMEM = pltpu.VMEM
LANES = 128


def peer(groups, k):
    me = lax.axis_index("rows")
    x = lax.rem(me // 16 + k // 16, groups // 16)
    y = lax.rem(lax.rem(me // 2, 8) + lax.rem(k, 8), 8)
    z = lax.rem(lax.rem(me, 2) + lax.rem(k // 8, 2), 2)
    return x * 16 + y * 2 + z


def each_peer(groups, action):
    def step(k, carry):
        action(peer(groups, k))
        return carry

    lax.fori_loop(1, groups, step, 0)


def to_row(source, landing, sends, receives, slot, there):
    return pltpu.make_async_remote_copy(
        src_ref=source,
        dst_ref=landing.at[slot],
        send_sem=sends.at[there],
        recv_sem=receives.at[slot],
        device_id={"rows": there},
        device_id_type=MESH,
    )


def greet_rows(groups):
    barrier = pltpu.get_barrier_semaphore()
    each_peer(
        groups,
        lambda there: pl.semaphore_signal(barrier, inc=1, device_id={"rows": there}, device_id_type=MESH),
    )
    return barrier


def trade_kernel(
    groups, mixed, answer, mixed_out, answer_out, relayed,
    sends, receives, answer_sends, answer_receives, relay_sends, relay_receives, own, hop,
):
    me = lax.axis_index("rows")
    along_x = groups // 16
    half = mixed.shape[3] // 2
    x = me // 16
    y = lax.rem(me // 2, 8)
    z = lax.rem(me, 2)
    pl.semaphore_wait(greet_rows(groups), groups - 1)

    def at_row(px, ky, pz):
        return px * 16 + lax.rem(y + ky, 8) * 2 + pz

    def chunk(there):
        return mixed.at[there // 16, lax.rem(there // 2, 8), lax.rem(there, 2)]

    def send(slot, there):
        return to_row(chunk(there), mixed_out, sends, receives, slot, there)

    def send_late_half(slot, there):
        return pltpu.make_async_remote_copy(
            src_ref=chunk(there).at[pl.ds(half, half)],
            dst_ref=mixed_out.at[slot, pl.ds(half, half)],
            send_sem=sends.at[there],
            recv_sem=receives.at[slot],
            device_id={"rows": there},
            device_id_type=MESH,
        )

    def send_answer(slot, there):
        return to_row(answer.at[there // 8], answer_out, answer_sends, answer_receives, slot, there)

    def every(send_one):
        def plane(j, carry):
            px = lax.rem(x + j // 2, along_x)
            pz = lax.rem(z + lax.rem(j, 2), 2)
            for ky in (4, 3, 5, 2, 6, 1, 7):
                there = at_row(px, ky, pz)
                send_one(send_late_half if ky == 4 else send, there)
                send_one(send_answer, there)
            return carry

        def level(j, carry):
            there = at_row(lax.rem(x + j // 2, along_x), 0, lax.rem(z + lax.rem(j, 2), 2))
            send_one(send, there)
            send_one(send_answer, there)
            return carry

        lax.fori_loop(0, 2 * along_x, plane, 0)
        lax.fori_loop(1, 2 * along_x, level, 0)

    to_relay = pltpu.make_async_remote_copy(
        src_ref=mixed.at[:, lax.rem(y + 4, 8), :, pl.ds(0, half)],
        dst_ref=relayed,
        send_sem=hop.at[0],
        recv_sem=hop.at[1],
        device_id={"rows": at_row(x, 6, z)},
        device_id_type=MESH,
    )
    to_relay.start()
    every(lambda copy, there: copy(me, there).start())
    keep = pltpu.make_async_copy(chunk(me), mixed_out.at[me], own.at[0])
    keep_answer = pltpu.make_async_copy(answer.at[me // 8], answer_out.at[me], own.at[1])
    keep.start()
    keep_answer.start()
    keep.wait()
    keep_answer.wait()
    to_relay.wait()

    def forward(j, slot, receive):
        px = j // 2
        pz = lax.rem(j, 2)
        return pltpu.make_async_remote_copy(
            src_ref=relayed.at[px, pz],
            dst_ref=mixed_out.at[slot, pl.ds(0, half)],
            send_sem=relay_sends.at[j],
            recv_sem=relay_receives.at[receive],
            device_id={"rows": at_row(px, 6, pz)},
            device_id_type=MESH,
        )

    def pass_on(j, carry):
        forward(j, at_row(x, 2, z), x * 2 + z).start()
        return carry

    def take(j, carry):
        forward(j, at_row(j // 2, 4, lax.rem(j, 2)), j).wait()
        return carry

    lax.fori_loop(0, 2 * along_x, pass_on, 0)
    every(lambda copy, there: copy(there, there).wait())
    lax.fori_loop(0, 2 * along_x, take, 0)


def trade(mixed, answer):
    groups, share, width = mixed.shape
    planes = 2 * (groups // 16)
    return pl.pallas_call(
        functools.partial(trade_kernel, groups),
        out_shape=[
            jax.ShapeDtypeStruct(mixed.shape, jnp.float32),
            jax.ShapeDtypeStruct((groups, 1, LANES), jnp.float32),
        ],
        in_specs=[pl.BlockSpec(memory_space=VMEM)] * 2,
        out_specs=[pl.BlockSpec(memory_space=VMEM)] * 2,
        scratch_shapes=[VMEM((groups // 16, 2, share // 2, width), jnp.float32)]
        + [pltpu.SemaphoreType.DMA((groups,))] * 4
        + [pltpu.SemaphoreType.DMA((planes,))] * 2
        + [pltpu.SemaphoreType.DMA((2,))] * 2,
        compiler_params=pltpu.CompilerParams(collective_id=0, has_side_effects=True),
    )(mixed.reshape(groups // 16, 8, 2, share, width), answer)


def mix_kernel(design, signs, response, mixed, answer):
    height, width = design.shape
    blocks = height // LANES
    h_lanes = sylvester(LANES, jnp.float32)
    flips = signs[...].astype(jnp.float32)
    for b in range(blocks):
        top, rest = halves(design[b * LANES:(b + 1) * LANES, :])
        matrix = (h_lanes * flips[b:b + 1, :]).astype(jnp.bfloat16)
        part = dot(matrix, top) + dot(matrix, rest)
        mixed[b * 8:(b + 1) * 8] = part.reshape(8, LANES // 8, width)

    def level(i, carry):
        row = lax.rem(i, 2) * 8
        values = butterfly([mixed[b * 8 + i // 2, pl.ds(row, 8), :] for b in range(blocks)])
        for b in range(blocks):
            mixed[b * 8 + i // 2, pl.ds(row, 8), :] = values[b]
        return carry

    lax.fori_loop(0, LANES // 8, level, 0)
    folded = jnp.dot(response[...] * flips, h_lanes, precision=lax.Precision.HIGHEST, preferred_element_type=jnp.float32)
    rows = butterfly([folded[b:b + 1, :] for b in range(blocks)])
    for b in range(blocks):
        answer[b] = rows[b]


def local_mix(design, signs, response):
    height, width = design.shape
    blocks = height // LANES
    return pl.pallas_call(
        mix_kernel,
        out_shape=[
            jax.ShapeDtypeStruct((64, height // 64, width), jnp.float32),
            jax.ShapeDtypeStruct((blocks, 1, LANES), jnp.float32),
        ],
        in_specs=[pl.BlockSpec(memory_space=VMEM)] * 3,
        out_specs=[pl.BlockSpec(memory_space=VMEM)] * 2,
    )(design, signs.reshape(blocks, LANES), response.reshape(blocks, LANES))


def gram_kernel(mixed, answer, picks, gram, small, held):
    groups, share, width = mixed.shape
    height = groups * share
    position = lax.axis_index("rows")

    def first(i, carry):
        row = lax.rem(i, 2) * 8
        values = butterfly([mixed[i // 2 * 8 + b, pl.ds(row, 8), :] for b in range(8)])
        for b in range(8):
            held[i // 2 * 8 + b, pl.ds(row, 8), :] = values[b]
        return carry

    def second(i, carry):
        row = lax.rem(i, 2) * 8
        values = butterfly([held[b * 8 + i // 2, pl.ds(row, 8), :] for b in range(8)])
        for b in range(8):
            held[b * 8 + i // 2, pl.ds(row, 8), :] = values[b]
        return carry

    lax.fori_loop(0, 16, first, 0)
    lax.fori_loop(0, 16, second, 0)
    mixed_answer = jnp.dot(
        sylvester(groups, jnp.float32), answer[:, 0, :],
        precision=lax.Precision.HIGHEST, preferred_element_type=jnp.float32,
    )
    wanted = picks[...]
    group_of = jnp.right_shift(wanted, 10)
    inside = jnp.bitwise_and(wanted, height - 1) - position * share
    samples = wanted.shape[1]
    of_group = (lax.broadcasted_iota(jnp.int32, (groups, samples), 0) == group_of).astype(jnp.float32)
    of_local = (lax.broadcasted_iota(jnp.int32, (LANES, samples), 0) == inside).astype(jnp.float32)
    picked = lax.dot_general(
        of_group.astype(jnp.bfloat16), of_local[:share].astype(jnp.bfloat16), (((1,), (1,)), ((), ())),
        preferred_element_type=jnp.float32,
    )
    lane = lax.broadcasted_iota(jnp.int32, (groups, share, share), 2)
    local_row = lax.broadcasted_iota(jnp.int32, (groups, share, share), 1)
    picked_rows = jnp.sum(jnp.where(lane == local_row, picked[:, None, :], 0.0), axis=2, keepdims=True)
    lane = lax.broadcasted_iota(jnp.int32, (groups, share, LANES), 2)
    local_row = lax.broadcasted_iota(jnp.int32, (groups, share, LANES), 1) + lax.rem(position, 8) * share
    answer_rows = jnp.sum(jnp.where(lane == local_row, mixed_answer[:, None, :], 0.0), axis=2, keepdims=True)
    picked_rows = picked_rows.reshape(height, 1)
    answer_rows = answer_rows.reshape(height, 1) * picked_rows

    chosen = held[...].reshape(height, width) * picked_rows
    top, rest = halves(chosen)

    def outer(left, right):
        return lax.dot_general(left, right, (((0,), (0,)), ((), ())), preferred_element_type=jnp.float32)

    total = outer(top, top) + outer(top, rest) + outer(rest, top)
    half = width // 2
    for h in range(2):
        gram[h] = total[:, h * half:(h + 1) * half].reshape(gram.shape[1:])
    rhs = jnp.sum(chosen * answer_rows, axis=0, keepdims=True)
    trace = jnp.sum(jnp.sum(chosen * chosen, axis=0, keepdims=True), axis=1, keepdims=True)
    power = jnp.sum(answer_rows * answer_rows, axis=0, keepdims=True)
    for j in range(width // LANES):
        small[j:j + 1, :] = rhs[:, j * LANES:(j + 1) * LANES]
    small[4:5, :] = jnp.broadcast_to(trace, (1, LANES))
    small[5:6, :] = jnp.broadcast_to(power, (1, LANES))
    small[6:8, :] = jnp.zeros((2, LANES), jnp.float32)


def local_gram(mixed, answer, picks):
    groups, share, width = mixed.shape
    return pl.pallas_call(
        gram_kernel,
        out_shape=[
            jax.ShapeDtypeStruct((2, groups // 16, 8, 2, width // groups, width // 2), jnp.float32),
            jax.ShapeDtypeStruct((8, LANES), jnp.float32),
        ],
        in_specs=[pl.BlockSpec(memory_space=VMEM)] * 3,
        out_specs=[pl.BlockSpec(memory_space=VMEM)] * 2,
        scratch_shapes=[VMEM(mixed.shape, jnp.float32)],
        compiler_params=pltpu.CompilerParams(vmem_limit_bytes=60 * 2**20),
    )(mixed, answer, picks.reshape(1, -1))


def finish_kernel(
    columns, samples, gram, small, gram_out, rhs_out,
    a_first, a_first_sum, a_second, a_second_sum, a_third,
    b_first, b_first_sum, b_second, b_second_sum, b_third,
    s_first, s_first_sum, s_second, s_second_sum, s_third,
    sends, receives,
):
    me = lax.axis_index("rows")
    column = lax.axis_index("cols")
    along_x = gram.shape[1]
    x = me // 16
    y = lax.rem(me // 2, 8)
    z = lax.rem(me, 2)
    other_z = 1 - z

    def row_at(kx, ky, kz):
        return lax.rem(x + kx, along_x) * 16 + lax.rem(y + ky, 8) * 2 + lax.rem(z + kz, 2)

    plane = [(kx, kz) for kz in range(2) for kx in range(along_x) if kx or kz]
    plane_rows = [row_at(kx, 0, kz) for kx, kz in plane]
    y_rows = [row_at(0, ky, 0) for ky in range(1, 8)]
    others = [lax.rem(column + k, columns) for k in range(1, columns)]

    barrier = pltpu.get_barrier_semaphore()
    for there in plane_rows + y_rows:
        pl.semaphore_signal(barrier, inc=1, device_id={"rows": there}, device_id_type=MESH)
    for there in others:
        pl.semaphore_signal(barrier, inc=1, device_id={"cols": there}, device_id_type=MESH)
    pl.semaphore_wait(barrier, len(plane_rows) + len(y_rows) + len(others))

    used = []

    def send(source, landing, **there):
        index = len(used)
        used.append(index)
        copy = pltpu.make_async_remote_copy(
            src_ref=source,
            dst_ref=landing,
            send_sem=sends.at[index],
            recv_sem=receives.at[index],
            device_id=there,
            device_id_type=MESH,
        )
        copy.start()
        return copy

    def wait(copies):
        for copy in copies:
            copy.wait()

    s1 = [send(small, s_first.at[k], rows=there) for k, there in enumerate(plane_rows)]
    b1 = [send(gram.at[1, :, :, other_z], b_first, rows=row_at(0, 0, 1))]
    a1 = [
        send(gram.at[0, lax.rem(x + k, along_x)], a_first.at[k - 1], rows=row_at(k, 0, 0))
        for k in (2, 1, 3)
    ]
    wait(s1)
    s_first_sum[...] = small[...] + jnp.sum(s_first[...], axis=0)
    s2 = [send(s_first_sum, s_second.at[k], rows=there) for k, there in enumerate(y_rows)]
    wait(b1)
    b_first_sum[...] = gram[1, :, :, z] + b_first[...]
    b2 = [
        send(b_first_sum.at[lax.rem(x + k, along_x)], b_second.at[k - 1], rows=row_at(k, 0, 0))
        for k in (2, 1, 3)
    ]
    wait(a1)
    a_first_sum[...] = gram[0, x] + a_first[0] + a_first[1] + a_first[2]
    a2 = [send(a_first_sum.at[:, other_z], a_second, rows=row_at(0, 0, 1))]
    wait(s2)
    s_second_sum[...] = s_first_sum[...] + jnp.sum(s_second[...], axis=0)
    s3 = [send(s_second_sum, s_third.at[k], cols=there) for k, there in enumerate(others)]
    wait(a2)
    a_second_sum[...] = a_first_sum[:, z] + a_second[...]
    a3 = [
        send(a_second_sum.at[lax.rem(y + k, 8)], a_third.at[k - 1], rows=y_rows[k - 1])
        for k in (4, 3, 5, 2, 6, 1, 7)
    ]
    wait(b2)
    b_second_sum[...] = b_first_sum[x] + b_second[0] + b_second[1] + b_second[2]
    b3 = [
        send(b_second_sum.at[lax.rem(y + k, 8)], b_third.at[k - 1], rows=y_rows[k - 1])
        for k in (4, 3, 5, 2, 6, 1, 7)
    ]
    wait(s3)
    mine = s_second_sum[...]
    mean_diag = (mine + jnp.sum(s_third[...], axis=0))[4:5, :] / D + epsilon
    scaled = mine * jnp.sqrt(jnp.float32(samples)) / jnp.sqrt(mean_diag * mine[5:6, :])
    rhs_out[...] = scaled[: BW // LANES, :]
    wait(a3)
    left = a_second_sum[y] + jnp.sum(a_third[...], axis=0)
    wait(b3)
    right = b_second_sum[y] + jnp.sum(b_third[...], axis=0)
    for half, block in enumerate((left, right)):
        for j in range(BW // 2 // LANES):
            at = half * (BW // 2) + j * LANES
            gram_out[:, at:at + LANES] = block[:, j * LANES:(j + 1) * LANES] / mean_diag


def finish(gram, small, columns, samples):
    _, nx, ny, nz, height, half = gram.shape
    count = 2 * (nx - 1) + 2 + 2 * (ny - 1) + (nx * nz - 1) + (ny - 1) + (columns - 1)

    def space(*shape):
        return VMEM(shape, jnp.float32)

    tile = small.shape
    return pl.pallas_call(
        functools.partial(finish_kernel, columns, samples),
        out_shape=[
            jax.ShapeDtypeStruct((height, 2 * half), jnp.float32),
            jax.ShapeDtypeStruct((BW // LANES, LANES), jnp.float32),
        ],
        in_specs=[pl.BlockSpec(memory_space=VMEM)] * 2,
        out_specs=[pl.BlockSpec(memory_space=VMEM)] * 2,
        scratch_shapes=[
            space(nx - 1, ny, nz, height, half), space(ny, nz, height, half),
            space(ny, height, half), space(ny, height, half), space(ny - 1, height, half),
            space(nx, ny, height, half), space(nx, ny, height, half),
            space(nx - 1, ny, height, half), space(ny, height, half), space(ny - 1, height, half),
            space(nx * nz - 1, *tile), space(*tile), space(ny - 1, *tile), space(*tile), space(columns - 1, *tile),
            pltpu.SemaphoreType.DMA((count,)),
            pltpu.SemaphoreType.DMA((count,)),
        ],
        compiler_params=pltpu.CompilerParams(collective_id=1, has_side_effects=True),
    )(gram, small)


def local(design, signs, response, picks):
    mixed, answer = trade(*local_mix(design, signs, response))
    gram, small = local_gram(mixed, answer, picks)
    gram_rows, rhs = finish(gram, small, lax.axis_size("cols"), picks.shape[0])
    return (gram_rows[:, None, :], rhs.reshape(BW))


def solution(mesh):
    in_specs = (P("rows", "cols"), P("rows"), P("rows"), P())
    out_specs = (P("rows", "cols", None), P("cols"))
    return jax.shard_map(local, mesh=mesh, in_specs=in_specs, out_specs=out_specs, check_vma=False)
```

```python
import functools

import jax
import jax.numpy as jnp
from jax import lax
from jax.experimental import pallas as pl
from jax.experimental.pallas import tpu as pltpu
from jax.sharding import PartitionSpec as P

D = 4096
BW = 512

epsilon = 1e-06


def sylvester(order, dtype):
    row_ids = lax.broadcasted_iota(jnp.int32, (order, order), 0)
    col_ids = lax.broadcasted_iota(jnp.int32, (order, order), 1)
    common = jnp.bitwise_and(row_ids, col_ids)
    return (1 - 2 * jnp.bitwise_and(lax.population_count(common), 1)).astype(dtype)


def halves(values):
    top = values.astype(jnp.bfloat16)
    return top, (values - top.astype(jnp.float32)).astype(jnp.bfloat16)


def dot(left, right):
    return jnp.dot(left, right, preferred_element_type=jnp.float32)


def butterfly(values):
    apart = 1
    while apart < len(values):
        values = [
            values[i ^ apart] - values[i] if i & apart else values[i] + values[i ^ apart]
            for i in range(len(values))
        ]
        apart *= 2
    return values


MESH = pl.DeviceIdType.MESH
VMEM = pltpu.VMEM
LANES = 128


def peer(groups, k):
    me = lax.axis_index("rows")
    x = lax.rem(me // 16 + k // 16, groups // 16)
    y = lax.rem(lax.rem(me // 2, 8) + lax.rem(k, 8), 8)
    z = lax.rem(lax.rem(me, 2) + lax.rem(k // 8, 2), 2)
    return x * 16 + y * 2 + z


def each_peer(groups, action):
    def step(k, carry):
        action(peer(groups, k))
        return carry

    lax.fori_loop(1, groups, step, 0)


def to_row(source, landing, sends, receives, slot, there):
    return pltpu.make_async_remote_copy(
        src_ref=source,
        dst_ref=landing.at[slot],
        send_sem=sends.at[there],
        recv_sem=receives.at[slot],
        device_id={"rows": there},
        device_id_type=MESH,
    )


def greet_rows(groups):
    barrier = pltpu.get_barrier_semaphore()
    each_peer(
        groups,
        lambda there: pl.semaphore_signal(barrier, inc=1, device_id={"rows": there}, device_id_type=MESH),
    )
    return barrier


def trade_kernel(
    groups, mixed, answer, picks, mixed_out, answer_out, picked,
    sends, receives, answer_sends, answer_receives, own,
):
    me = lax.axis_index("rows")
    share = mixed.shape[1]
    pl.semaphore_wait(greet_rows(groups), groups - 1)

    def start(there):
        to_row(mixed.at[there], mixed_out, sends, receives, me, there).start()
        to_row(answer.at[there // 8], answer_out, answer_sends, answer_receives, me, there).start()

    def finish(there):
        to_row(mixed.at[there], mixed_out, sends, receives, there, there).wait()
        to_row(answer.at[there // 8], answer_out, answer_sends, answer_receives, there, there).wait()

    each_peer(groups, start)
    keep = pltpu.make_async_copy(mixed.at[me], mixed_out.at[me], own.at[0])
    keep_answer = pltpu.make_async_copy(answer.at[me // 8], answer_out.at[me], own.at[1])
    keep.start()
    keep_answer.start()
    wanted = picks[...]
    group_of = jnp.right_shift(wanted, 10)
    inside = jnp.bitwise_and(wanted, groups * share - 1) - me * share
    samples = wanted.shape[1]
    of_group = (lax.broadcasted_iota(jnp.int32, (groups, samples), 0) == group_of).astype(jnp.float32)
    of_local = (lax.broadcasted_iota(jnp.int32, (share, samples), 0) == inside).astype(jnp.float32)
    picked[...] = lax.dot_general(
        of_group.astype(jnp.bfloat16), of_local.astype(jnp.bfloat16), (((1,), (1,)), ((), ())),
        preferred_element_type=jnp.float32,
    )
    keep.wait()
    keep_answer.wait()
    each_peer(groups, finish)


def trade(mixed, answer, picks):
    groups = mixed.shape[0]
    return pl.pallas_call(
        functools.partial(trade_kernel, groups),
        out_shape=[
            jax.ShapeDtypeStruct(mixed.shape, jnp.float32),
            jax.ShapeDtypeStruct((groups, 1, LANES), jnp.float32),
            jax.ShapeDtypeStruct((groups, mixed.shape[1]), jnp.float32),
        ],
        in_specs=[pl.BlockSpec(memory_space=VMEM)] * 3,
        out_specs=[pl.BlockSpec(memory_space=VMEM)] * 3,
        scratch_shapes=[pltpu.SemaphoreType.DMA((groups,))] * 4 + [pltpu.SemaphoreType.DMA((2,))],
        compiler_params=pltpu.CompilerParams(collective_id=0, has_side_effects=True),
    )(mixed, answer, picks.reshape(1, -1))


def mix_kernel(design, signs, response, mixed, answer):
    height, width = design.shape
    blocks = height // LANES
    h_lanes = sylvester(LANES, jnp.float32)
    flips = signs[...].astype(jnp.float32)
    for b in range(blocks):
        top, rest = halves(design[b * LANES:(b + 1) * LANES, :])
        matrix = (h_lanes * flips[b:b + 1, :]).astype(jnp.bfloat16)
        part = dot(matrix, top) + dot(matrix, rest)
        mixed[b * 8:(b + 1) * 8] = part.reshape(8, LANES // 8, width)

    def level(i, carry):
        row = lax.rem(i, 2) * 8
        values = butterfly([mixed[b * 8 + i // 2, pl.ds(row, 8), :] for b in range(blocks)])
        for b in range(blocks):
            mixed[b * 8 + i // 2, pl.ds(row, 8), :] = values[b]
        return carry

    lax.fori_loop(0, LANES // 8, level, 0)
    folded = jnp.dot(response[...] * flips, h_lanes, precision=lax.Precision.HIGHEST, preferred_element_type=jnp.float32)
    rows = butterfly([folded[b:b + 1, :] for b in range(blocks)])
    for b in range(blocks):
        answer[b] = rows[b]


def local_mix(design, signs, response):
    height, width = design.shape
    blocks = height // LANES
    return pl.pallas_call(
        mix_kernel,
        out_shape=[
            jax.ShapeDtypeStruct((64, height // 64, width), jnp.float32),
            jax.ShapeDtypeStruct((blocks, 1, LANES), jnp.float32),
        ],
        in_specs=[pl.BlockSpec(memory_space=VMEM)] * 3,
        out_specs=[pl.BlockSpec(memory_space=VMEM)] * 2,
    )(design, signs.reshape(blocks, LANES), response.reshape(blocks, LANES))


def gram_kernel(mixed, answer, picked, gram, small, held):
    groups, share, width = mixed.shape
    height = groups * share
    position = lax.axis_index("rows")

    def first(i, carry):
        row = lax.rem(i, 2) * 8
        values = butterfly([mixed[i // 2 * 8 + b, pl.ds(row, 8), :] for b in range(8)])
        for b in range(8):
            held[i // 2 * 8 + b, pl.ds(row, 8), :] = values[b]
        return carry

    def second(i, carry):
        row = lax.rem(i, 2) * 8
        values = butterfly([held[b * 8 + i // 2, pl.ds(row, 8), :] for b in range(8)])
        for b in range(8):
            held[b * 8 + i // 2, pl.ds(row, 8), :] = values[b]
        return carry

    lax.fori_loop(0, 16, first, 0)
    lax.fori_loop(0, 16, second, 0)
    mixed_answer = jnp.dot(
        sylvester(groups, jnp.float32), answer[:, 0, :],
        precision=lax.Precision.HIGHEST, preferred_element_type=jnp.float32,
    )
    lane = lax.broadcasted_iota(jnp.int32, (groups, share, share), 2)
    local_row = lax.broadcasted_iota(jnp.int32, (groups, share, share), 1)
    picked_rows = jnp.sum(jnp.where(lane == local_row, picked[...][:, None, :], 0.0), axis=2, keepdims=True)
    lane = lax.broadcasted_iota(jnp.int32, (groups, share, LANES), 2)
    local_row = lax.broadcasted_iota(jnp.int32, (groups, share, LANES), 1) + lax.rem(position, 8) * share
    answer_rows = jnp.sum(jnp.where(lane == local_row, mixed_answer[:, None, :], 0.0), axis=2, keepdims=True)
    picked_rows = picked_rows.reshape(height, 1)
    answer_rows = answer_rows.reshape(height, 1) * picked_rows

    chosen = held[...].reshape(height, width) * picked_rows
    top, rest = halves(chosen)

    def outer(left, right):
        return lax.dot_general(left, right, (((0,), (0,)), ((), ())), preferred_element_type=jnp.float32)

    total = outer(top, top) + outer(top, rest) + outer(rest, top)
    half = width // 2
    for h in range(2):
        gram[h] = total[:, h * half:(h + 1) * half].reshape(gram.shape[1:])
    rhs = jnp.sum(chosen * answer_rows, axis=0, keepdims=True)
    trace = jnp.sum(jnp.sum(chosen * chosen, axis=0, keepdims=True), axis=1, keepdims=True)
    power = jnp.sum(answer_rows * answer_rows, axis=0, keepdims=True)
    for j in range(width // LANES):
        small[j:j + 1, :] = rhs[:, j * LANES:(j + 1) * LANES]
    small[4:5, :] = jnp.broadcast_to(trace, (1, LANES))
    small[5:6, :] = jnp.broadcast_to(power, (1, LANES))
    small[6:8, :] = jnp.zeros((2, LANES), jnp.float32)


def local_gram(mixed, answer, picked):
    groups, share, width = mixed.shape
    return pl.pallas_call(
        gram_kernel,
        out_shape=[
            jax.ShapeDtypeStruct((2, groups // 16, 8, 2, width // groups, width // 2), jnp.float32),
            jax.ShapeDtypeStruct((8, LANES), jnp.float32),
        ],
        in_specs=[pl.BlockSpec(memory_space=VMEM)] * 3,
        out_specs=[pl.BlockSpec(memory_space=VMEM)] * 2,
        scratch_shapes=[VMEM(mixed.shape, jnp.float32)],
        compiler_params=pltpu.CompilerParams(vmem_limit_bytes=60 * 2**20),
    )(mixed, answer, picked)


def finish_kernel(
    columns, samples, gram, small, gram_out, rhs_out,
    a_first, a_first_sum, a_second, a_second_sum, a_third,
    b_first, b_first_sum, b_second, b_second_sum, b_third,
    s_first, s_first_sum, s_second, s_second_sum, s_third,
    sends, receives,
):
    me = lax.axis_index("rows")
    column = lax.axis_index("cols")
    along_x = gram.shape[1]
    x = me // 16
    y = lax.rem(me // 2, 8)
    z = lax.rem(me, 2)
    other_z = 1 - z

    def row_at(kx, ky, kz):
        return lax.rem(x + kx, along_x) * 16 + lax.rem(y + ky, 8) * 2 + lax.rem(z + kz, 2)

    plane = [(kx, kz) for kz in range(2) for kx in range(along_x) if kx or kz]
    plane_rows = [row_at(kx, 0, kz) for kx, kz in plane]
    y_rows = [row_at(0, ky, 0) for ky in range(1, 8)]
    others = [lax.rem(column + k, columns) for k in range(1, columns)]

    barrier = pltpu.get_barrier_semaphore()
    for there in plane_rows + y_rows:
        pl.semaphore_signal(barrier, inc=1, device_id={"rows": there}, device_id_type=MESH)
    for there in others:
        pl.semaphore_signal(barrier, inc=1, device_id={"cols": there}, device_id_type=MESH)
    pl.semaphore_wait(barrier, len(plane_rows) + len(y_rows) + len(others))

    used = []

    def send(source, landing, **there):
        index = len(used)
        used.append(index)
        copy = pltpu.make_async_remote_copy(
            src_ref=source,
            dst_ref=landing,
            send_sem=sends.at[index],
            recv_sem=receives.at[index],
            device_id=there,
            device_id_type=MESH,
        )
        copy.start()
        return copy

    def wait(copies):
        for copy in copies:
            copy.wait()

    s1 = [send(small, s_first.at[k], rows=there) for k, there in enumerate(plane_rows)]
    b1 = [send(gram.at[1, :, :, other_z], b_first, rows=row_at(0, 0, 1))]
    a1 = [
        send(gram.at[0, lax.rem(x + k, along_x)], a_first.at[k - 1], rows=row_at(k, 0, 0))
        for k in (2, 1, 3)
    ]
    wait(s1)
    s_first_sum[...] = small[...] + jnp.sum(s_first[...], axis=0)
    s2 = [send(s_first_sum, s_second.at[k], rows=there) for k, there in enumerate(y_rows)]
    wait(b1)
    b_first_sum[...] = gram[1, :, :, z] + b_first[...]
    b2 = [
        send(b_first_sum.at[lax.rem(x + k, along_x)], b_second.at[k - 1], rows=row_at(k, 0, 0))
        for k in (2, 1, 3)
    ]
    wait(a1)
    a_first_sum[...] = gram[0, x] + a_first[0] + a_first[1] + a_first[2]
    a2 = [send(a_first_sum.at[:, other_z], a_second, rows=row_at(0, 0, 1))]
    wait(s2)
    s_second_sum[...] = s_first_sum[...] + jnp.sum(s_second[...], axis=0)
    s3 = [send(s_second_sum, s_third.at[k], cols=there) for k, there in enumerate(others)]
    wait(a2)
    a_second_sum[...] = a_first_sum[:, z] + a_second[...]
    a3 = [
        send(a_second_sum.at[lax.rem(y + k, 8)], a_third.at[k - 1], rows=y_rows[k - 1])
        for k in (4, 3, 5, 2, 6, 1, 7)
    ]
    wait(b2)
    b_second_sum[...] = b_first_sum[x] + b_second[0] + b_second[1] + b_second[2]
    b3 = [
        send(b_second_sum.at[lax.rem(y + k, 8)], b_third.at[k - 1], rows=y_rows[k - 1])
        for k in (4, 3, 5, 2, 6, 1, 7)
    ]
    wait(s3)
    mine = s_second_sum[...]
    mean_diag = (mine + jnp.sum(s_third[...], axis=0))[4:5, :] / D + epsilon
    scaled = mine * jnp.sqrt(jnp.float32(samples)) / jnp.sqrt(mean_diag * mine[5:6, :])
    rhs_out[...] = scaled[: BW // LANES, :]
    wait(a3)
    left = a_second_sum[y] + jnp.sum(a_third[...], axis=0)
    wait(b3)
    right = b_second_sum[y] + jnp.sum(b_third[...], axis=0)
    for half, block in enumerate((left, right)):
        for j in range(BW // 2 // LANES):
            at = half * (BW // 2) + j * LANES
            gram_out[:, at:at + LANES] = block[:, j * LANES:(j + 1) * LANES] / mean_diag


def finish(gram, small, columns, samples):
    _, nx, ny, nz, height, half = gram.shape
    count = 2 * (nx - 1) + 2 + 2 * (ny - 1) + (nx * nz - 1) + (ny - 1) + (columns - 1)

    def space(*shape):
        return VMEM(shape, jnp.float32)

    tile = small.shape
    return pl.pallas_call(
        functools.partial(finish_kernel, columns, samples),
        out_shape=[
            jax.ShapeDtypeStruct((height, 2 * half), jnp.float32),
            jax.ShapeDtypeStruct((BW // LANES, LANES), jnp.float32),
        ],
        in_specs=[pl.BlockSpec(memory_space=VMEM)] * 2,
        out_specs=[pl.BlockSpec(memory_space=VMEM)] * 2,
        scratch_shapes=[
            space(nx - 1, ny, nz, height, half), space(ny, nz, height, half),
            space(ny, height, half), space(ny, height, half), space(ny - 1, height, half),
            space(nx, ny, height, half), space(nx, ny, height, half),
            space(nx - 1, ny, height, half), space(ny, height, half), space(ny - 1, height, half),
            space(nx * nz - 1, *tile), space(*tile), space(ny - 1, *tile), space(*tile), space(columns - 1, *tile),
            pltpu.SemaphoreType.DMA((count,)),
            pltpu.SemaphoreType.DMA((count,)),
        ],
        compiler_params=pltpu.CompilerParams(collective_id=1, has_side_effects=True),
    )(gram, small)


def local(design, signs, response, picks):
    mixed, answer, picked = trade(*local_mix(design, signs, response), picks)
    gram, small = local_gram(mixed, answer, picked)
    gram_rows, rhs = finish(gram, small, lax.axis_size("cols"), picks.shape[0])
    return (gram_rows[:, None, :], rhs.reshape(BW))


def solution(mesh):
    in_specs = (P("rows", "cols"), P("rows"), P("rows"), P())
    out_specs = (P("rows", "cols", None), P("cols"))
    return jax.shard_map(local, mesh=mesh, in_specs=in_specs, out_specs=out_specs, check_vma=False)
```

```python
import functools

import jax
import jax.numpy as jnp
from jax import lax
from jax.experimental import pallas as pl
from jax.experimental.pallas import tpu as pltpu
from jax.sharding import PartitionSpec as P

D = 4096
BW = 512

epsilon = 1e-06


def sylvester(order, dtype):
    row_ids = lax.broadcasted_iota(jnp.int32, (order, order), 0)
    col_ids = lax.broadcasted_iota(jnp.int32, (order, order), 1)
    common = jnp.bitwise_and(row_ids, col_ids)
    return (1 - 2 * jnp.bitwise_and(lax.population_count(common), 1)).astype(dtype)


def halves(values):
    top = values.astype(jnp.bfloat16)
    return top, (values - top.astype(jnp.float32)).astype(jnp.bfloat16)


def dot(left, right):
    return jnp.dot(left, right, preferred_element_type=jnp.float32)


def butterfly(values):
    apart = 1
    while apart < len(values):
        values = [
            values[i ^ apart] - values[i] if i & apart else values[i] + values[i ^ apart]
            for i in range(len(values))
        ]
        apart *= 2
    return values


MESH = pl.DeviceIdType.MESH
VMEM = pltpu.VMEM
LANES = 128


def peer(groups, k):
    me = lax.axis_index("rows")
    x = lax.rem(me // 16 + k // 16, groups // 16)
    y = lax.rem(lax.rem(me // 2, 8) + lax.rem(k, 8), 8)
    z = lax.rem(lax.rem(me, 2) + lax.rem(k // 8, 2), 2)
    return x * 16 + y * 2 + z


def each_peer(groups, action):
    def step(k, carry):
        action(peer(groups, lax.rem(k * 27, groups)))
        return carry

    lax.fori_loop(1, groups, step, 0)


def to_row(source, landing, sends, receives, slot, there):
    return pltpu.make_async_remote_copy(
        src_ref=source,
        dst_ref=landing.at[slot],
        send_sem=sends.at[there],
        recv_sem=receives.at[slot],
        device_id={"rows": there},
        device_id_type=MESH,
    )


def greet_rows(groups):
    barrier = pltpu.get_barrier_semaphore()
    each_peer(
        groups,
        lambda there: pl.semaphore_signal(barrier, inc=1, device_id={"rows": there}, device_id_type=MESH),
    )
    return barrier


def trade_kernel(
    groups, mixed, answer, picks, mixed_out, answer_out, picked,
    sends, receives, answer_sends, answer_receives, own,
):
    me = lax.axis_index("rows")
    share = mixed.shape[1]
    pl.semaphore_wait(greet_rows(groups), groups - 1)

    def start(there):
        to_row(mixed.at[there], mixed_out, sends, receives, me, there).start()
        to_row(answer.at[there // 8], answer_out, answer_sends, answer_receives, me, there).start()

    def finish(there):
        to_row(mixed.at[there], mixed_out, sends, receives, there, there).wait()
        to_row(answer.at[there // 8], answer_out, answer_sends, answer_receives, there, there).wait()

    each_peer(groups, start)
    keep = pltpu.make_async_copy(mixed.at[me], mixed_out.at[me], own.at[0])
    keep_answer = pltpu.make_async_copy(answer.at[me // 8], answer_out.at[me], own.at[1])
    keep.start()
    keep_answer.start()
    wanted = picks[...]
    group_of = jnp.right_shift(wanted, 10)
    inside = jnp.bitwise_and(wanted, groups * share - 1) - me * share
    samples = wanted.shape[1]
    of_group = (lax.broadcasted_iota(jnp.int32, (groups, samples), 0) == group_of).astype(jnp.float32)
    of_local = (lax.broadcasted_iota(jnp.int32, (share, samples), 0) == inside).astype(jnp.float32)
    picked[...] = lax.dot_general(
        of_group.astype(jnp.bfloat16), of_local.astype(jnp.bfloat16), (((1,), (1,)), ((), ())),
        preferred_element_type=jnp.float32,
    )
    keep.wait()
    keep_answer.wait()
    each_peer(groups, finish)


def trade(mixed, answer, picks):
    groups = mixed.shape[0]
    return pl.pallas_call(
        functools.partial(trade_kernel, groups),
        out_shape=[
            jax.ShapeDtypeStruct(mixed.shape, jnp.float32),
            jax.ShapeDtypeStruct((groups, 1, LANES), jnp.float32),
            jax.ShapeDtypeStruct((groups, mixed.shape[1]), jnp.float32),
        ],
        in_specs=[pl.BlockSpec(memory_space=VMEM)] * 3,
        out_specs=[pl.BlockSpec(memory_space=VMEM)] * 3,
        scratch_shapes=[pltpu.SemaphoreType.DMA((groups,))] * 4 + [pltpu.SemaphoreType.DMA((2,))],
        compiler_params=pltpu.CompilerParams(collective_id=0, has_side_effects=True),
    )(mixed, answer, picks.reshape(1, -1))


def mix_kernel(design, signs, response, mixed, answer):
    height, width = design.shape
    blocks = height // LANES
    h_lanes = sylvester(LANES, jnp.float32)
    flips = signs[...].astype(jnp.float32)
    for b in range(blocks):
        top, rest = halves(design[b * LANES:(b + 1) * LANES, :])
        matrix = (h_lanes * flips[b:b + 1, :]).astype(jnp.bfloat16)
        part = dot(matrix, top) + dot(matrix, rest)
        mixed[b * 8:(b + 1) * 8] = part.reshape(8, LANES // 8, width)

    def level(i, carry):
        row = lax.rem(i, 2) * 8
        values = butterfly([mixed[b * 8 + i // 2, pl.ds(row, 8), :] for b in range(blocks)])
        for b in range(blocks):
            mixed[b * 8 + i // 2, pl.ds(row, 8), :] = values[b]
        return carry

    lax.fori_loop(0, LANES // 8, level, 0)
    folded = jnp.dot(response[...] * flips, h_lanes, precision=lax.Precision.HIGHEST, preferred_element_type=jnp.float32)
    rows = butterfly([folded[b:b + 1, :] for b in range(blocks)])
    for b in range(blocks):
        answer[b] = rows[b]


def local_mix(design, signs, response):
    height, width = design.shape
    blocks = height // LANES
    return pl.pallas_call(
        mix_kernel,
        out_shape=[
            jax.ShapeDtypeStruct((64, height // 64, width), jnp.float32),
            jax.ShapeDtypeStruct((blocks, 1, LANES), jnp.float32),
        ],
        in_specs=[pl.BlockSpec(memory_space=VMEM)] * 3,
        out_specs=[pl.BlockSpec(memory_space=VMEM)] * 2,
    )(design, signs.reshape(blocks, LANES), response.reshape(blocks, LANES))


def gram_kernel(mixed, answer, picked, gram, small, held):
    groups, share, width = mixed.shape
    height = groups * share
    position = lax.axis_index("rows")

    def first(i, carry):
        row = lax.rem(i, 2) * 8
        values = butterfly([mixed[i // 2 * 8 + b, pl.ds(row, 8), :] for b in range(8)])
        for b in range(8):
            held[i // 2 * 8 + b, pl.ds(row, 8), :] = values[b]
        return carry

    def second(i, carry):
        row = lax.rem(i, 2) * 8
        values = butterfly([held[b * 8 + i // 2, pl.ds(row, 8), :] for b in range(8)])
        for b in range(8):
            held[b * 8 + i // 2, pl.ds(row, 8), :] = values[b]
        return carry

    lax.fori_loop(0, 16, first, 0)
    lax.fori_loop(0, 16, second, 0)
    mixed_answer = jnp.dot(
        sylvester(groups, jnp.float32), answer[:, 0, :],
        precision=lax.Precision.HIGHEST, preferred_element_type=jnp.float32,
    )
    lane = lax.broadcasted_iota(jnp.int32, (groups, share, share), 2)
    local_row = lax.broadcasted_iota(jnp.int32, (groups, share, share), 1)
    picked_rows = jnp.sum(jnp.where(lane == local_row, picked[...][:, None, :], 0.0), axis=2, keepdims=True)
    lane = lax.broadcasted_iota(jnp.int32, (groups, share, LANES), 2)
    local_row = lax.broadcasted_iota(jnp.int32, (groups, share, LANES), 1) + lax.rem(position, 8) * share
    answer_rows = jnp.sum(jnp.where(lane == local_row, mixed_answer[:, None, :], 0.0), axis=2, keepdims=True)
    picked_rows = picked_rows.reshape(height, 1)
    answer_rows = answer_rows.reshape(height, 1) * picked_rows

    chosen = held[...].reshape(height, width) * picked_rows
    top, rest = halves(chosen)

    def outer(left, right):
        return lax.dot_general(left, right, (((0,), (0,)), ((), ())), preferred_element_type=jnp.float32)

    total = outer(top, top) + outer(top, rest) + outer(rest, top)
    half = width // 2
    for h in range(2):
        gram[h] = total[:, h * half:(h + 1) * half].reshape(gram.shape[1:])
    rhs = jnp.sum(chosen * answer_rows, axis=0, keepdims=True)
    trace = jnp.sum(jnp.sum(chosen * chosen, axis=0, keepdims=True), axis=1, keepdims=True)
    power = jnp.sum(answer_rows * answer_rows, axis=0, keepdims=True)
    for j in range(width // LANES):
        small[j:j + 1, :] = rhs[:, j * LANES:(j + 1) * LANES]
    small[4:5, :] = jnp.broadcast_to(trace, (1, LANES))
    small[5:6, :] = jnp.broadcast_to(power, (1, LANES))
    small[6:8, :] = jnp.zeros((2, LANES), jnp.float32)


def local_gram(mixed, answer, picked):
    groups, share, width = mixed.shape
    return pl.pallas_call(
        gram_kernel,
        out_shape=[
            jax.ShapeDtypeStruct((2, groups // 16, 8, 2, width // groups, width // 2), jnp.float32),
            jax.ShapeDtypeStruct((8, LANES), jnp.float32),
        ],
        in_specs=[pl.BlockSpec(memory_space=VMEM)] * 3,
        out_specs=[pl.BlockSpec(memory_space=VMEM)] * 2,
        scratch_shapes=[VMEM(mixed.shape, jnp.float32)],
        compiler_params=pltpu.CompilerParams(vmem_limit_bytes=60 * 2**20),
    )(mixed, answer, picked)


def finish_kernel(
    columns, samples, gram, small, gram_out, rhs_out,
    a_first, a_first_sum, a_second, a_second_sum, a_third,
    b_first, b_first_sum, b_second, b_second_sum, b_third,
    s_first, s_first_sum, s_second, s_second_sum, s_third,
    sends, receives,
):
    me = lax.axis_index("rows")
    column = lax.axis_index("cols")
    along_x = gram.shape[1]
    x = me // 16
    y = lax.rem(me // 2, 8)
    z = lax.rem(me, 2)
    other_z = 1 - z

    def row_at(kx, ky, kz):
        return lax.rem(x + kx, along_x) * 16 + lax.rem(y + ky, 8) * 2 + lax.rem(z + kz, 2)

    plane = [(kx, kz) for kz in range(2) for kx in range(along_x) if kx or kz]
    plane_rows = [row_at(kx, 0, kz) for kx, kz in plane]
    y_rows = [row_at(0, ky, 0) for ky in range(1, 8)]
    others = [lax.rem(column + k, columns) for k in range(1, columns)]

    barrier = pltpu.get_barrier_semaphore()
    for there in plane_rows + y_rows:
        pl.semaphore_signal(barrier, inc=1, device_id={"rows": there}, device_id_type=MESH)
    for there in others:
        pl.semaphore_signal(barrier, inc=1, device_id={"cols": there}, device_id_type=MESH)
    pl.semaphore_wait(barrier, len(plane_rows) + len(y_rows) + len(others))

    used = []

    def send(source, landing, **there):
        index = len(used)
        used.append(index)
        copy = pltpu.make_async_remote_copy(
            src_ref=source,
            dst_ref=landing,
            send_sem=sends.at[index],
            recv_sem=receives.at[index],
            device_id=there,
            device_id_type=MESH,
        )
        copy.start()
        return copy

    def wait(copies):
        for copy in copies:
            copy.wait()

    s1 = [send(small, s_first.at[k], rows=there) for k, there in enumerate(plane_rows)]
    b1 = [send(gram.at[1, :, :, other_z], b_first, rows=row_at(0, 0, 1))]
    a1 = [
        send(gram.at[0, lax.rem(x + k, along_x)], a_first.at[k - 1], rows=row_at(k, 0, 0))
        for k in (2, 1, 3)
    ]
    wait(s1)
    s_first_sum[...] = small[...] + jnp.sum(s_first[...], axis=0)
    s2 = [send(s_first_sum, s_second.at[k], rows=there) for k, there in enumerate(y_rows)]
    wait(b1)
    b_first_sum[...] = gram[1, :, :, z] + b_first[...]
    b2 = [
        send(b_first_sum.at[lax.rem(x + k, along_x)], b_second.at[k - 1], rows=row_at(k, 0, 0))
        for k in (2, 1, 3)
    ]
    wait(a1)
    a_first_sum[...] = gram[0, x] + a_first[0] + a_first[1] + a_first[2]
    a2 = [send(a_first_sum.at[:, other_z], a_second, rows=row_at(0, 0, 1))]
    wait(s2)
    s_second_sum[...] = s_first_sum[...] + jnp.sum(s_second[...], axis=0)
    s3 = [send(s_second_sum, s_third.at[k], cols=there) for k, there in enumerate(others)]
    wait(a2)
    a_second_sum[...] = a_first_sum[:, z] + a_second[...]
    a3 = [
        send(a_second_sum.at[lax.rem(y + k, 8)], a_third.at[k - 1], rows=y_rows[k - 1])
        for k in (4, 3, 5, 2, 6, 1, 7)
    ]
    wait(b2)
    b_second_sum[...] = b_first_sum[x] + b_second[0] + b_second[1] + b_second[2]
    b3 = [
        send(b_second_sum.at[lax.rem(y + k, 8)], b_third.at[k - 1], rows=y_rows[k - 1])
        for k in (4, 3, 5, 2, 6, 1, 7)
    ]
    wait(s3)
    mine = s_second_sum[...]
    mean_diag = (mine + jnp.sum(s_third[...], axis=0))[4:5, :] / D + epsilon
    scaled = mine * jnp.sqrt(jnp.float32(samples)) / jnp.sqrt(mean_diag * mine[5:6, :])
    rhs_out[...] = scaled[: BW // LANES, :]
    wait(a3)
    left = a_second_sum[y] + jnp.sum(a_third[...], axis=0)
    wait(b3)
    right = b_second_sum[y] + jnp.sum(b_third[...], axis=0)
    for half, block in enumerate((left, right)):
        for j in range(BW // 2 // LANES):
            at = half * (BW // 2) + j * LANES
            gram_out[:, at:at + LANES] = block[:, j * LANES:(j + 1) * LANES] / mean_diag


def finish(gram, small, columns, samples):
    _, nx, ny, nz, height, half = gram.shape
    count = 2 * (nx - 1) + 2 + 2 * (ny - 1) + (nx * nz - 1) + (ny - 1) + (columns - 1)

    def space(*shape):
        return VMEM(shape, jnp.float32)

    tile = small.shape
    return pl.pallas_call(
        functools.partial(finish_kernel, columns, samples),
        out_shape=[
            jax.ShapeDtypeStruct((height, 2 * half), jnp.float32),
            jax.ShapeDtypeStruct((BW // LANES, LANES), jnp.float32),
        ],
        in_specs=[pl.BlockSpec(memory_space=VMEM)] * 2,
        out_specs=[pl.BlockSpec(memory_space=VMEM)] * 2,
        scratch_shapes=[
            space(nx - 1, ny, nz, height, half), space(ny, nz, height, half),
            space(ny, height, half), space(ny, height, half), space(ny - 1, height, half),
            space(nx, ny, height, half), space(nx, ny, height, half),
            space(nx - 1, ny, height, half), space(ny, height, half), space(ny - 1, height, half),
            space(nx * nz - 1, *tile), space(*tile), space(ny - 1, *tile), space(*tile), space(columns - 1, *tile),
            pltpu.SemaphoreType.DMA((count,)),
            pltpu.SemaphoreType.DMA((count,)),
        ],
        compiler_params=pltpu.CompilerParams(collective_id=1, has_side_effects=True),
    )(gram, small)


def local(design, signs, response, picks):
    mixed, answer, picked = trade(*local_mix(design, signs, response), picks)
    gram, small = local_gram(mixed, answer, picked)
    gram_rows, rhs = finish(gram, small, lax.axis_size("cols"), picks.shape[0])
    return (gram_rows[:, None, :], rhs.reshape(BW))


def solution(mesh):
    in_specs = (P("rows", "cols"), P("rows"), P("rows"), P())
    out_specs = (P("rows", "cols", None), P("cols"))
    return jax.shard_map(local, mesh=mesh, in_specs=in_specs, out_specs=out_specs, check_vma=False)
```
